128 devices in a mesh: term: 32 (over y_lo, x, z), pair: 4 (over y_hi, core).
Axes of the slice: x: 4, y: 4 (y_hi: 2, y_lo: 2; y = y_hi * 2 + y_lo), z: 4, core: 2. Of those that a mesh axis runs over, the one named last changes fastest.
Arguments:
- core_rows: bfloat16 [12288, 256], P(('term', 'pair')), may hold values from -0.25 to 0.25
- norm_ops: bfloat16 [2048, 512, 512], P(('term', 'pair')), may hold values from -6 to 6
- norm_sectors: int32 [2048, 2], P(('term', 'pair')), may hold values from 0 to 23
- comp_ops: bfloat16 [2048, 512, 512], P(('term', 'pair')), may hold values from -1.5 to 1.5
- comp_sectors: int32 [2048, 2], P(('term', 'pair')), may hold values from 0 to 23
- comp_group: int32 [2048, 1], P(('term', 'pair')), may hold values from 0 to 3; in each aligned block of 16 rows (0 to 15, 16 to 31, ...) at most 8 rows name the same one
- comp_slot: int32 [2048], P(('term', 'pair')), may hold values from 0 to 31
Outputs:
- normal_rotated: bfloat16 [2048, 256, 256], P(('term', 'pair'))
- comp_rotated: bfloat16 [4, 32, 256, 256], P('pair', 'term')
The draws below stay inside these ranges and needn't reach their ends.
Inputs may be any that keep to these rules, and one draw needn't show every extreme that they name: `comp_group`: among the complementary tiles of one device (aligned blocks of 16 rows), at most 8 name the same owner group, a bound that some block reaches of them.
All inputs are finite; a program needn't handle non-finite values.
Results may differ from the reference program's by a relative error of at most 0.017.
Values may be sent and summed in bfloat16 or wider, within the bound.
No kernel may reach another device: no remote copies, remote signals or barrier semaphores. Data moves between devices by JAX's collectives and lax.ppermute only.
A program may use at most 128 MiB of HBM per device.

```python
import math
import jax
import jax.numpy as jnp
import numpy as np
from jax import lax

TILE = 256
SECTORS = 24
COMP_DEV = 16
KT = 512
CAP = 8
NORM_ALL = 2048
COMP_ALL = 2048
OWNED = 32
N_TERM = 32
N_PAIR = 4


def with_ends(result, stream_key, least, high):
    index_at = [jax.random.randint(jax.random.fold_in(stream_key, axis), (), 0, length) for axis, length in enumerate(result.shape)]
    widest = result.shape.index(max(result.shape))
    neighbour = index_at[:widest] + [(index_at[widest] + 1) % result.shape[widest]] + index_at[widest + 1:]
    return result.at[tuple(index_at)].set(least).at[tuple(neighbour)].set(high)


def levels(key, dims, cuts, smallest, largest):
    level, own = 1.0, jax.random.fold_in(key, 6)
    for dim, blocks in cuts:
        draws = jnp.exp(jax.random.uniform(jax.random.fold_in(own, dim), (blocks,), jnp.float32, smallest / len(cuts), largest / len(cuts)))
        level = level * jnp.repeat(draws, dims[dim] // blocks).reshape([-1 if axis == dim else 1 for axis in range(len(dims))])
    return level


def deal_out(rng, own, number, rows, count, top, limit, slope):
    ranking = jax.random.permutation(rng, count)
    heavy_load, ordinary = portions_of(count, rows * top, limit, slope, True), portions_of(count, rows * top, limit, slope, False)
    places = jnp.arange(count)

    def named(lengths, rotation):
        used = int((lengths > 0).sum())
        fixed = max(1, used // 4)
        passed = fixed + (places - fixed + rotation * (used - fixed)) % max(1, count - fixed)
        return jnp.zeros((count,), jnp.int32).at[ranking[jnp.where(places < fixed, places, passed)]].set(jnp.asarray(lengths, jnp.int32))

    lengths = jnp.where(number % 4 == 0, named(heavy_load, number // 4), named(ordinary, number - number // 4 - 1))
    mixed = jax.random.permutation(jax.random.fold_in(own, 3), count)
    giver, sink = mixed[0:count // 2 * 2:2], mixed[1:count // 2 * 2:2]
    margin = jnp.minimum(lengths[giver] - 1, limit - lengths[sink]) // 2
    margin = jnp.where((giver == ranking[0]) | (sink == ranking[0]) | (lengths[sink] == 0), 0, jnp.maximum(margin, 0))
    passed = jax.random.randint(jax.random.fold_in(own, 4), (count // 2,), 0, 1 << 20) % (margin + 1)
    lengths = lengths.at[giver].add(-passed).at[sink].add(passed)
    labels = jnp.searchsorted(jnp.cumsum(lengths), jnp.arange(rows * top), side="right").astype(jnp.int32)
    table = labels.reshape(top, rows).T
    table = table[jax.random.permutation(jax.random.fold_in(own, 1), rows)]
    rotation = jax.random.randint(jax.random.fold_in(own, 2), (rows, 1), 0, top)
    return jnp.take_along_axis(table, (jnp.arange(top)[None, :] + rotation) % top, axis=1)


def portions_of(amount, total, limit, lean, full):
    portions = [(1 << 20) // math.isqrt(standing ** lean) + 1 for standing in range(1, amount + 1)]
    largest = limit if full else min(limit, max(-(-total // amount), total * portions[0] // sum(portions)))
    least = 1 if total - largest >= amount - 1 else 0
    holding, spare = [largest] + [least] * (amount - 1), total - largest - least * (amount - 1)
    while spare > 0:
        movable = [i for i in range(1, amount) if holding[i] < largest] or [i for i in range(1, amount) if holding[i] < limit]
        mass, remaining = sum([portions[i] for i in movable]), spare
        for i in movable:
            addition = min(limit - holding[i], max(1, remaining * portions[i] // mass), spare)
            holding[i] = holding[i] + addition
            spare = spare - addition
    return np.array(holding)


def scatter_about(rng, dims, deviation, most, cuts=(), dtype=jnp.bfloat16):
    loudness = levels(rng, dims, cuts, -0.22, 0.18) if cuts else 1.0
    array = jax.random.normal(rng, dims, jnp.float32) * deviation * loudness
    return jnp.minimum(jnp.maximum(array, -most), most).astype(dtype)


def setup_inputs(seed: int = 0) -> dict:
    keys = jax.random.split(jax.random.key(seed), 8)
    core_rows = scatter_about(keys[0], (SECTORS * KT, TILE), KT ** -0.5, 0.25, ((0, 128),))
    norm_ops = scatter_about(keys[1], (NORM_ALL, KT, KT), 1.0, 6.0, ((0, 128),))
    norm_sectors = with_ends(jax.random.randint(keys[2], (NORM_ALL, 2), 0, SECTORS), jax.random.fold_in(keys[2], 1), 0, SECTORS - 1).astype(jnp.int32)
    comp_ops = scatter_about(keys[3], (COMP_ALL, KT, KT), 0.25, 1.5, ((0, 128),))
    comp_sectors = with_ends(jax.random.randint(keys[4], (COMP_ALL, 2), 0, SECTORS), jax.random.fold_in(keys[4], 1), 0, SECTORS - 1).astype(jnp.int32)
    comp_group_keys = jax.random.split(jax.random.fold_in(keys[5], 1), COMP_ALL // COMP_DEV)
    comp_group_turns = jax.random.permutation(jax.random.fold_in(keys[5], 3), COMP_ALL // COMP_DEV)
    comp_group = jax.vmap(lambda own, number: deal_out(jax.random.fold_in(keys[5], 2), own, number, COMP_DEV, N_PAIR, 1, CAP, 2))(comp_group_keys, comp_group_turns).reshape((COMP_ALL, 1))
    comp_slot = with_ends(jax.random.randint(keys[6], (COMP_ALL,), 0, OWNED), jax.random.fold_in(keys[6], 1), 0, OWNED - 1).astype(jnp.int32)
    return dict(core_rows=core_rows, norm_ops=norm_ops, norm_sectors=norm_sectors, comp_ops=comp_ops, comp_sectors=comp_sectors, comp_group=comp_group, comp_slot=comp_slot)


def rotate_tiles(core_tiles, op_tiles, sector_ids):
    left_rot = core_tiles[sector_ids[:, 0]].astype(jnp.float32)
    right_rot = core_tiles[sector_ids[:, 1]].astype(jnp.float32)
    half_rotated = jnp.einsum('nab,nbc->nac', op_tiles.astype(jnp.float32), right_rot).astype(jnp.bfloat16)
    half_rotated = lax.optimization_barrier(half_rotated).astype(jnp.float32)
    return jnp.einsum('nba,nbc->nac', left_rot, half_rotated)


def reference(core_rows, norm_ops, norm_sectors, comp_ops, comp_sectors, comp_group, comp_slot):
    core_tiles = core_rows.reshape(SECTORS, KT, TILE)

    def normal_block(inputs):
        return rotate_tiles(core_tiles, inputs[0], inputs[1]).astype(jnp.bfloat16)

    normal_rotated = lax.map(normal_block, (norm_ops.reshape(-1, 8, KT, KT), norm_sectors.reshape(-1, 8, 2)))
    normal_rotated = normal_rotated.reshape(NORM_ALL, TILE, TILE)
    targets = (comp_group[:, 0] * OWNED + comp_slot).astype(jnp.int32)

    def comp_block(total, inputs):
        rotated = rotate_tiles(core_tiles, inputs[0], inputs[1]).astype(jnp.bfloat16)
        rotated = lax.optimization_barrier(rotated).astype(jnp.float32)
        return total.at[inputs[2]].add(rotated), None

    def term_block(total, inputs):
        start_part = jnp.zeros((N_PAIR * OWNED, TILE, TILE), jnp.float32)
        part_sum, unused = lax.scan(comp_block, start_part, inputs)
        part_sum = lax.optimization_barrier(part_sum.astype(jnp.bfloat16)).astype(jnp.float32)
        return total + part_sum, None

    start_total = jnp.zeros((N_PAIR * OWNED, TILE, TILE), jnp.float32)
    blocks_per_term = (N_PAIR * COMP_DEV) // 8
    total, unused = lax.scan(term_block, start_total, (comp_ops.reshape(N_TERM, blocks_per_term, 8, KT, KT), comp_sectors.reshape(N_TERM, blocks_per_term, 8, 2), targets.reshape(N_TERM, blocks_per_term, 8)))
    comp_rotated = total.reshape(N_PAIR, OWNED, TILE, TILE).astype(jnp.bfloat16)
    return (normal_rotated, comp_rotated)
```

```python
import functools

import jax
import jax.numpy as jnp
from jax import lax
from jax.experimental import pallas as pl
from jax.experimental.pallas import tpu as pltpu
from jax.sharding import Mesh
from jax.sharding import PartitionSpec as P

AXES = ("ylo", "x", "z", "yhi", "core")
SIZES = (2, 4, 4, 2, 2)
TERM = ("ylo", "x", "z")
CHIPS = ("ylo", "x", "z", "yhi")
CHUNKS = 1


def rotate_kernel(chunks, sectors, place, core, own_ref, other_ref, op_ref, out_ref, u_ref, sem):
    step = pl.program_id(0)
    blocks, block_rows, _ = own_ref.shape

    @pl.when(step == 0)
    def _():
        mine = core[0]

        def copies(j):
            first = pl.multiple_of((2 * j + mine) * block_rows, 32)
            second = pl.multiple_of((2 * j + 1 - mine) * block_rows, 32)
            return (
                pltpu.make_async_copy(own_ref.at[j], u_ref.at[pl.ds(first, block_rows)], sem),
                pltpu.make_async_copy(other_ref.at[j], u_ref.at[pl.ds(second, block_rows)], sem),
            )

        @pl.loop(0, blocks)
        def _(j):
            for copy in copies(j):
                copy.start()

        @pl.loop(0, blocks)
        def _(j):
            for copy in copies(j):
                copy.wait()

    depth = op_ref.shape[1]
    left = u_ref[pl.ds(pl.multiple_of(sectors[step, 0] * depth, depth), depth), :]
    right = u_ref[pl.ds(pl.multiple_of(sectors[step, 1] * depth, depth), depth), :]
    half = jnp.dot(op_ref[0], right, preferred_element_type=jnp.float32).astype(jnp.bfloat16)
    full = lax.dot_general(
        left, half, (((0,), (0,)), ((), ())), preferred_element_type=jnp.float32
    ).astype(jnp.bfloat16)
    rows = full.shape[0] // chunks
    for k in range(chunks):
        out_ref[k, 0] = full[k * rows : (k + 1) * rows]


def rotate(own, other, core, ops, sectors, place, slots, chunks):
    count, depth, _ = ops.shape
    width = own.shape[2]
    rows = width // chunks
    return pl.pallas_call(
        functools.partial(rotate_kernel, chunks),
        out_shape=jax.ShapeDtypeStruct((chunks, slots, rows, width), jnp.bfloat16),
        grid_spec=pltpu.PrefetchScalarGridSpec(
            num_scalar_prefetch=3,
            grid=(count,),
            in_specs=[
                pl.BlockSpec(memory_space=pl.ANY),
                pl.BlockSpec(memory_space=pl.ANY),
                pl.BlockSpec((1, depth, depth), lambda i, s, p, c: (i, 0, 0)),
            ],
            out_specs=pl.BlockSpec((chunks, 1, rows, width), lambda i, s, p, c: (0, p[i], 0, 0)),
            scratch_shapes=[
                pltpu.VMEM((2 * own.shape[0] * own.shape[1], width), jnp.bfloat16),
                pltpu.SemaphoreType.DMA,
            ],
        ),
        cost_estimate=pl.CostEstimate(
            flops=count * 2 * depth * width * (depth + width),
            bytes_accessed=2 * (count * depth * depth + 2 * own.size + count * width * width),
            transcendentals=0,
        ),
    )(sectors, place, core, own, other, ops)


def combine_kernel(order, start, tiles_ref, out_ref):
    slots, rows, width = out_ref.shape
    piece = 64 if rows >= 64 else rows

    @pl.loop(0, slots)
    def _(p):
        for r in range(0, rows, piece):

            def add(j, total):
                return total + tiles_ref[order[j], r : r + piece, :].astype(jnp.float32)

            total = lax.fori_loop(
                start[p], start[p + 1], add, jnp.zeros((piece, width), jnp.float32)
            )
            out_ref[p, r : r + piece, :] = total.astype(jnp.bfloat16)


def combine(tiles, order, start, slots):
    _, rows, width = tiles.shape
    return pl.pallas_call(
        combine_kernel,
        out_shape=jax.ShapeDtypeStruct((slots, rows, width), jnp.bfloat16),
        grid_spec=pltpu.PrefetchScalarGridSpec(
            num_scalar_prefetch=2,
            grid=(1,),
            in_specs=[pl.BlockSpec(tiles.shape, lambda i, o, s: (0, 0, 0))],
            out_specs=pl.BlockSpec((slots, rows, width), lambda i, o, s: (0, 0, 0)),
        ),
        cost_estimate=pl.CostEstimate(
            flops=tiles.size, bytes_accessed=4 * tiles.size, transcendentals=0
        ),
    )(order, start, tiles)


def exchange(x, axes):
    return lax.all_to_all(x, axes, split_axis=0, concat_axis=0, tiled=True)


def on_device(core_rows, norm_ops, norm_sectors, comp_ops, comp_sectors, comp_group, comp_slot):
    width = core_rows.shape[1]
    count = comp_ops.shape[0]
    groups = lax.axis_size("yhi") * lax.axis_size("core")
    terms = lax.axis_size(TERM)
    chips = lax.axis_size(CHIPS)
    capacity = count // 2

    own = exchange(jnp.broadcast_to(core_rows[None], (chips, *core_rows.shape)), CHIPS)
    other = lax.ppermute(own, "core", [(0, 1), (1, 0)])
    core = lax.axis_index("core").reshape(1).astype(jnp.int32)

    group = comp_group[:, 0]
    member = group[:, None] == jnp.arange(groups, dtype=jnp.int32)[None, :]
    earlier = jnp.arange(count)[:, None] > jnp.arange(count)[None, :]
    rank = jnp.sum((group[:, None] == group[None, :]) & earlier, axis=1, dtype=jnp.int32)
    place = group * capacity + rank
    sent = groups * capacity
    dispatch = place[None, :] == jnp.arange(sent, dtype=jnp.int32)[:, None]
    slots_out = jnp.sum(jnp.where(dispatch, comp_slot[None, :] + 1, 0), axis=1) - 1
    slots_in = exchange(slots_out.reshape(groups, capacity), ("yhi", "core")).reshape(sent)
    key = jnp.where(slots_in < 0, terms, slots_in)
    j = jnp.arange(sent, dtype=jnp.int32)
    before = (key[None, :] < key[:, None]) | ((key[None, :] == key[:, None]) & (j[None, :] < j[:, None]))
    at = jnp.sum(before, axis=1, dtype=jnp.int32)
    order = jnp.sum(jnp.where(at[None, :] == j[:, None], j[None, :], 0), axis=1, dtype=jnp.int32)
    start = jnp.sum(
        key[None, :] < jnp.arange(terms + 1, dtype=jnp.int32)[:, None], axis=1, dtype=jnp.int32
    )

    outgoing = rotate(own, other, core, comp_ops, comp_sectors, place, sent, CHUNKS)
    pieces = []
    for k in range(CHUNKS):
        received = exchange(outgoing[k], ("yhi", "core"))
        partial = combine(received, order, start, terms)
        parts = exchange(partial, TERM)
        pieces.append(jnp.sum(parts.astype(jnp.float32), axis=0).astype(jnp.bfloat16))
    comp_rotated = jnp.concatenate(pieces, axis=0).reshape(1, 1, width, width)

    ids = jnp.arange(norm_ops.shape[0], dtype=jnp.int32)
    normal = rotate(own, other, core, norm_ops, norm_sectors, ids, norm_ops.shape[0], 1)
    return normal.reshape(-1, width, width), comp_rotated


def solution(mesh):
    cut = Mesh(mesh.devices.reshape(SIZES), AXES)
    every = AXES
    return jax.shard_map(
        on_device,
        mesh=cut,
        in_specs=(
            P(every, None),
            P(every, None, None),
            P(every, None),
            P(every, None, None),
            P(every, None),
            P(every, None),
            P(every),
        ),
        out_specs=(P(every, None, None), P(("yhi", "core"), TERM, None, None)),
        check_vma=False,
    )
```

```python
import functools

import jax
import jax.numpy as jnp
import numpy as np
from jax import lax
from jax.experimental import pallas as pl
from jax.experimental.pallas import tpu as pltpu
from jax.sharding import Mesh
from jax.sharding import PartitionSpec as P

AXES = ("ylo", "x", "z", "yhi", "core")
SIZES = (2, 4, 4, 2, 2)
TERM = ("ylo", "x", "z")
CHIPS = ("ylo", "x", "z", "yhi")
CHUNKS = 2
TILES_PER_STEP = 4


def peers(flip_y, flip_core):
    pairs = []
    for i in range(int(np.prod(SIZES))):
        ylo, x, z, yhi, core = np.unravel_index(i, SIZES)
        there = (ylo ^ flip_y, x, z, yhi ^ flip_y, core ^ flip_core)
        pairs.append((i, int(np.ravel_multi_index(there, SIZES))))
    return pairs


PEERS = (None, peers(0, 1), peers(1, 0), peers(1, 1))


def rotate_kernel(chunks, split, capacity, *refs):
    sectors, place, core, own_ref, other_ref, op_ref = refs[:6]
    out_refs = refs[6 : 6 + chunks * split]
    u_ref, res_ref, load_sem, store_sem = refs[6 + chunks * split :]
    step = pl.program_id(0)
    blocks, block_rows, _ = own_ref.shape
    tiles, depth, _ = op_ref.shape
    rows = res_ref.shape[2]

    @pl.when(step == 0)
    def _():
        mine = core[0]

        def copies(j):
            first = pl.multiple_of((2 * j + mine) * block_rows, 32)
            second = pl.multiple_of((2 * j + 1 - mine) * block_rows, 32)
            return (
                pltpu.make_async_copy(own_ref.at[j], u_ref.at[pl.ds(first, block_rows)], load_sem),
                pltpu.make_async_copy(other_ref.at[j], u_ref.at[pl.ds(second, block_rows)], load_sem),
            )

        @pl.loop(0, blocks)
        def _(j):
            for copy in copies(j):
                copy.start()

        @pl.loop(0, blocks)
        def _(j):
            for copy in copies(j):
                copy.wait()

    def sector(i, side):
        return u_ref[pl.ds(pl.multiple_of(sectors[i, side] * depth, depth), depth), :]

    def store(i, k, m):
        return pltpu.make_async_copy(
            res_ref.at[k, i], out_refs[k * split + m].at[place[i] % capacity], store_sem
        )

    halves = [
        jnp.dot(op_ref[t], sector(step * tiles + t, 1), preferred_element_type=jnp.float32).astype(
            jnp.bfloat16
        )
        for t in range(tiles)
    ]
    for t in range(tiles):
        i = step * tiles + t
        full = lax.dot_general(
            sector(i, 0), halves[t], (((0,), (0,)), ((), ())), preferred_element_type=jnp.float32
        ).astype(jnp.bfloat16)
        for k in range(chunks):
            res_ref[k, i] = full[k * rows : (k + 1) * rows]
    for t in range(tiles):
        i = step * tiles + t
        for m in range(split):

            @pl.when(place[i] // capacity == m)
            def _(i=i, m=m):
                for k in range(chunks):
                    store(i, k, m).start()

    @pl.when(step == pl.num_programs(0) - 1)
    def _():
        @pl.loop(0, pl.num_programs(0) * tiles)
        def _(i):
            for k in range(chunks):
                store(i, k, 0).wait()


def rotate(own, other, core, ops, sectors, place, capacity, split, chunks):
    count, depth, _ = ops.shape
    width = own.shape[2]
    rows = width // chunks
    tiles = TILES_PER_STEP
    return pl.pallas_call(
        functools.partial(rotate_kernel, chunks, split, capacity),
        out_shape=[jax.ShapeDtypeStruct((capacity, rows, width), jnp.bfloat16)] * (chunks * split),
        grid_spec=pltpu.PrefetchScalarGridSpec(
            num_scalar_prefetch=3,
            grid=(count // tiles,),
            in_specs=[
                pl.BlockSpec(memory_space=pl.ANY),
                pl.BlockSpec(memory_space=pl.ANY),
                pl.BlockSpec((tiles, depth, depth), lambda i, s, p, c: (i, 0, 0)),
            ],
            out_specs=[pl.BlockSpec(memory_space=pl.ANY)] * (chunks * split),
            scratch_shapes=[
                pltpu.VMEM((2 * own.shape[0] * own.shape[1], width), jnp.bfloat16),
                pltpu.VMEM((chunks, count, rows, width), jnp.bfloat16),
                pltpu.SemaphoreType.DMA,
                pltpu.SemaphoreType.DMA,
            ],
        ),
        cost_estimate=pl.CostEstimate(
            flops=count * 2 * depth * width * (depth + width),
            bytes_accessed=2 * (count * depth * depth + 2 * own.size + count * width * width),
            transcendentals=0,
        ),
    )(sectors, place, core, own, other, ops)


def combine_kernel(order, start, *refs):
    *in_refs, out_ref, tiles_ref, sem = refs
    slots, rows, width = out_ref.shape
    capacity = in_refs[0].shape[0]
    copies = [
        pltpu.make_async_copy(ref, tiles_ref.at[pl.ds(m * capacity, capacity)], sem.at[m])
        for m, ref in enumerate(in_refs)
    ]
    for copy in copies:
        copy.start()
    for copy in copies:
        copy.wait()
    piece = min(rows, 64)

    @pl.loop(0, slots)
    def _(p):
        for r in range(0, rows, piece):

            def add(j, total):
                return total + tiles_ref[order[j], r : r + piece, :].astype(jnp.float32)

            total = lax.fori_loop(
                start[p], start[p + 1], add, jnp.zeros((piece, width), jnp.float32)
            )
            out_ref[p, r : r + piece, :] = total.astype(jnp.bfloat16)


def combine(received, order, start, slots):
    capacity, rows, width = received[0].shape
    held = len(received) * capacity
    return pl.pallas_call(
        combine_kernel,
        out_shape=jax.ShapeDtypeStruct((slots, rows, width), jnp.bfloat16),
        grid_spec=pltpu.PrefetchScalarGridSpec(
            num_scalar_prefetch=2,
            grid=(1,),
            in_specs=[pl.BlockSpec(memory_space=pl.ANY)] * len(received),
            out_specs=pl.BlockSpec((slots, rows, width), lambda i, o, s: (0, 0, 0)),
            scratch_shapes=[
                pltpu.VMEM((held, rows, width), jnp.bfloat16),
                pltpu.SemaphoreType.DMA((len(received),)),
            ],
        ),
        cost_estimate=pl.CostEstimate(
            flops=held * rows * width,
            bytes_accessed=2 * (held + slots) * rows * width,
            transcendentals=0,
        ),
    )(order, start, *received)


def exchange(x, axes):
    return lax.all_to_all(x, axes, split_axis=0, concat_axis=0, tiled=True)


def on_device(core_rows, norm_ops, norm_sectors, comp_ops, comp_sectors, comp_group, comp_slot):
    width = core_rows.shape[1]
    count = comp_ops.shape[0]
    groups = len(PEERS)
    terms = lax.axis_size(TERM)
    chips = lax.axis_size(CHIPS)
    capacity = count // 2

    own = exchange(jnp.broadcast_to(core_rows[None], (chips, *core_rows.shape)), CHIPS)
    other = lax.ppermute(own, "core", [(0, 1), (1, 0)])
    core = lax.axis_index("core").reshape(1).astype(jnp.int32)

    group = comp_group[:, 0]
    mine = lax.axis_index(("yhi", "core")).astype(jnp.int32)
    earlier = jnp.arange(count)[:, None] > jnp.arange(count)[None, :]
    rank = jnp.sum((group[:, None] == group[None, :]) & earlier, axis=1, dtype=jnp.int32)
    place = (group ^ mine) * capacity + rank
    sent = groups * capacity
    dispatch = place[None, :] == jnp.arange(sent, dtype=jnp.int32)[:, None]
    slots_out = jnp.sum(jnp.where(dispatch, comp_slot[None, :] + 1, 0), axis=1) - 1

    outgoing = rotate(
        own, other, core, comp_ops, comp_sectors, place, capacity, groups, CHUNKS
    )
    slots_out, outgoing = lax.optimization_barrier((slots_out, outgoing))

    def send(arrays):
        return [
            a if pairs is None else lax.ppermute(a, AXES, pairs)
            for a, pairs in zip(arrays, PEERS, strict=True)
        ]

    received = [send(outgoing[k * groups : (k + 1) * groups]) for k in range(CHUNKS)]
    slots_in = jnp.concatenate(send(list(slots_out.reshape(groups, capacity))))
    key = jnp.where(slots_in < 0, terms, slots_in)
    j = jnp.arange(sent, dtype=jnp.int32)
    before = (key[None, :] < key[:, None]) | (
        (key[None, :] == key[:, None]) & (j[None, :] < j[:, None])
    )
    at = jnp.sum(before, axis=1, dtype=jnp.int32)
    order = jnp.sum(jnp.where(at[None, :] == j[:, None], j[None, :], 0), axis=1, dtype=jnp.int32)
    start = jnp.sum(
        key[None, :] < jnp.arange(terms + 1, dtype=jnp.int32)[:, None], axis=1, dtype=jnp.int32
    )

    pieces = []
    for k in range(CHUNKS):
        partial = combine(received[k], order, start, terms)
        parts = exchange(partial, TERM)
        pieces.append(jnp.sum(parts.astype(jnp.float32), axis=0).astype(jnp.bfloat16))
    comp_rotated = jnp.concatenate(pieces, axis=0).reshape(1, 1, width, width)

    held = norm_ops.shape[0]
    ids = jnp.arange(held, dtype=jnp.int32)
    (normal,) = rotate(own, other, core, norm_ops, norm_sectors, ids, held, 1, 1)
    return normal, comp_rotated


def solution(mesh):
    cut = Mesh(mesh.devices.reshape(SIZES), AXES)
    return jax.shard_map(
        on_device,
        mesh=cut,
        in_specs=(
            P(AXES, None),
            P(AXES, None, None),
            P(AXES, None),
            P(AXES, None, None),
            P(AXES, None),
            P(AXES, None),
            P(AXES),
        ),
        out_specs=(P(AXES, None, None), P(("yhi", "core"), TERM, None, None)),
        check_vma=False,
    )
```

```python
import functools

import jax
import jax.numpy as jnp
import numpy as np
from jax import lax
from jax.experimental import pallas as pl
from jax.experimental.pallas import tpu as pltpu
from jax.sharding import Mesh
from jax.sharding import PartitionSpec as P


AXES = ("ylo", "x", "z", "yhi", "core")
SIZES = (2, 4, 4, 2, 2)
TERM = ("ylo", "x", "z")
PLANE = ("x", "z")
CHUNKS = (48, 80, 128)
TILES_PER_STEP = 4


def peers(flip_y, flip_core):
    pairs = []
    for i in range(int(np.prod(SIZES))):
        ylo, x, z, yhi, core = np.unravel_index(i, SIZES)
        there = (ylo ^ flip_y, x, z, yhi ^ flip_y, core ^ flip_core)
        pairs.append((i, int(np.ravel_multi_index(there, SIZES))))
    return pairs


def up(step):
    pairs = []
    for i in range(int(np.prod(SIZES))):
        ylo, x, z, yhi, core = np.unravel_index(i, SIZES)
        y = (2 * yhi + ylo + step) % 4
        pairs.append((i, int(np.ravel_multi_index((y % 2, x, z, y // 2, core), SIZES))))
    return pairs


PEERS = (None, peers(0, 1), peers(1, 0), peers(1, 1))


PIECES = ((0, 0, 16), (3, 0, 8), (1, 8, 8), (3, 8, 8), (1, 0, 8), (2, 0, 8), (2, 8, 8))


def rotate_kernel(chunks, split, capacity, *refs):
    sectors, place, where = refs[:3]
    piece_refs, op_ref = refs[3 : 3 + 2 * len(PIECES)], refs[3 + 2 * len(PIECES)]
    rest = refs[4 + 2 * len(PIECES) :]
    out_refs = rest[: len(chunks) * split]
    u_ref, res_ref, load_sem, store_sem = rest[len(chunks) * split :]
    step = pl.program_id(0)
    block_rows = piece_refs[0].shape[1]
    tiles, depth, _ = op_ref.shape

    @pl.when(step == 0)
    def _():
        def each(act):
            for n, ref in enumerate(piece_refs):
                ahead, first, count = PIECES[n % len(PIECES)]
                core = where[1] if n < len(PIECES) else 1 - where[1]
                y = lax.rem(where[0] + ahead, 4)
                base = lax.rem(y, 2) * 64 + (y // 2) * 2 + core

                @pl.loop(0, count)
                def _(j, ref=ref, first=first, base=base):
                    row = pl.multiple_of((base + (first + j) * 4) * block_rows, 32)
                    act(
                        pltpu.make_async_copy(
                            ref.at[j], u_ref.at[pl.ds(row, block_rows)], load_sem
                        )
                    )

        each(lambda copy: copy.start())
        each(lambda copy: copy.wait())

    def sector(i, side):
        return u_ref[pl.ds(pl.multiple_of(sectors[i, side] * depth, depth), depth), :]

    def stores(i, m):
        first = 0
        for k, rows in enumerate(chunks):
            yield pltpu.make_async_copy(
                res_ref.at[i, pl.ds(first, rows)],
                out_refs[k * split + m].at[place[i] % capacity],
                store_sem,
            )
            first += rows

    halves = [
        jnp.dot(op_ref[t], sector(step * tiles + t, 1), preferred_element_type=jnp.float32).astype(
            jnp.bfloat16
        )
        for t in range(tiles)
    ]
    for t in range(tiles):
        i = step * tiles + t
        res_ref[i] = lax.dot_general(
            sector(i, 0), halves[t], (((0,), (0,)), ((), ())), preferred_element_type=jnp.float32
        ).astype(jnp.bfloat16)
    for t in range(tiles):
        i = step * tiles + t
        for m in range(split):

            @pl.when(place[i] // capacity == m)
            def _(i=i, m=m):
                for copy in stores(i, m):
                    copy.start()

    @pl.when(step == pl.num_programs(0) - 1)
    def _():
        @pl.loop(0, pl.num_programs(0) * tiles)
        def _(i):
            for copy in stores(i, 0):
                copy.wait()


def rotate(held, where, ops, sectors, place, capacity, split, chunks):
    count, depth, _ = ops.shape
    block_rows, width = held[0].shape[1:]
    whole = sum(a.shape[0] for a in held) * block_rows
    tiles = TILES_PER_STEP
    shapes = [
        jax.ShapeDtypeStruct((capacity, rows, width), jnp.bfloat16)
        for rows in chunks
        for _ in range(split)
    ]
    return pl.pallas_call(
        functools.partial(rotate_kernel, chunks, split, capacity),
        out_shape=shapes,
        grid_spec=pltpu.PrefetchScalarGridSpec(
            num_scalar_prefetch=3,
            grid=(count // tiles,),
            in_specs=[
                *[pl.BlockSpec(memory_space=pl.ANY)] * len(held),
                pl.BlockSpec((tiles, depth, depth), lambda i, s, p, c: (i, 0, 0)),
            ],
            out_specs=[pl.BlockSpec(memory_space=pltpu.HBM)] * len(shapes),
            scratch_shapes=[
                pltpu.VMEM((whole, width), jnp.bfloat16),
                pltpu.VMEM((count, width, width), jnp.bfloat16),
                pltpu.SemaphoreType.DMA,
                pltpu.SemaphoreType.DMA,
            ],
        ),
        compiler_params=pltpu.CompilerParams(vmem_limit_bytes=56 << 20),
        cost_estimate=pl.CostEstimate(
            flops=count * 2 * depth * width * (depth + width),
            bytes_accessed=2 * (count * depth * depth + whole * width + count * width * width),
            transcendentals=0,
        ),
    )(sectors, place, where, *held, ops)


def combine_kernel(slots, *refs):
    *in_refs, out_ref, total_ref = refs
    capacity = in_refs[0].shape[0]
    total_ref[...] = jnp.zeros_like(total_ref)
    for m, ref in enumerate(in_refs):

        @pl.loop(0, capacity)
        def _(j, m=m, ref=ref):
            slot = slots[m * capacity + j]

            @pl.when(slot >= 0)
            def _():
                total_ref[slot] += ref[j].astype(jnp.float32)

    out_ref[...] = total_ref[...].astype(out_ref.dtype)


def combine(received, slots_in, slots):
    capacity, rows, width = received[0].shape
    held = len(received) * capacity
    return pl.pallas_call(
        combine_kernel,
        out_shape=jax.ShapeDtypeStruct((slots, rows, width), jnp.bfloat16),
        grid_spec=pltpu.PrefetchScalarGridSpec(
            num_scalar_prefetch=1,
            grid=(1,),
            in_specs=[
                pl.BlockSpec((capacity, rows, width), lambda i, s: (0, 0, 0)),
                *[pl.BlockSpec(memory_space=pltpu.VMEM)] * (len(received) - 1),
            ],
            out_specs=pl.BlockSpec(memory_space=pltpu.VMEM),
            scratch_shapes=[pltpu.VMEM((slots, rows, width), jnp.float32)],
        ),
        compiler_params=pltpu.CompilerParams(vmem_limit_bytes=24 << 20),
        cost_estimate=pl.CostEstimate(
            flops=held * rows * width,
            bytes_accessed=2 * (held + slots) * rows * width,
            transcendentals=0,
        ),
    )(slots_in, *received)


def exchange(x, axes):
    return lax.all_to_all(x, axes, split_axis=0, concat_axis=0, tiled=True)


def step(core_rows, norm_ops, norm_sectors, comp_ops, comp_sectors, comp_group, comp_slot):
    width = core_rows.shape[1]
    count = comp_ops.shape[0]
    groups = len(PEERS)
    terms = lax.axis_size(TERM)
    capacity = count // 2

    plane = lax.axis_size(PLANE)
    here = exchange(jnp.broadcast_to(core_rows[None], (plane, *core_rows.shape)), PLANE)
    low, high = here[: plane // 2], here[plane // 2 :]
    below_low, above_high = lax.ppermute(low, AXES, up(1)), lax.ppermute(high, AXES, up(-1))
    below_high, above_low = lax.ppermute(high, AXES, up(1)), lax.ppermute(low, AXES, up(-1))
    far_low, far_high = (
        lax.ppermute(below_low, AXES, up(1)),
        lax.ppermute(above_high, AXES, up(-1)),
    )
    own = [here, below_low, above_high, below_high, above_low, far_low, far_high]
    other = []
    for piece in own:
        other.append(lax.ppermute(piece, "core", [(0, 1), (1, 0)]))
    held = own + other
    y = 2 * lax.axis_index("yhi") + lax.axis_index("ylo")
    where = jnp.stack([y, lax.axis_index("core")]).astype(jnp.int32)

    group = comp_group[:, 0]
    mine = lax.axis_index(("yhi", "core")).astype(jnp.int32)
    earlier = jnp.arange(count)[:, None] > jnp.arange(count)[None, :]
    rank = jnp.sum((group[:, None] == group[None, :]) & earlier, axis=1, dtype=jnp.int32)
    place = (group ^ mine) * capacity + rank
    dispatch = place[None, :] == jnp.arange(groups * capacity, dtype=jnp.int32)[:, None]
    slots_out = jnp.sum(jnp.where(dispatch, comp_slot[None, :] + 1, 0), axis=1) - 1

    def send(arrays):
        sent = [
            lax.ppermute(a, AXES, pairs) for a, pairs in reversed(list(zip(arrays, PEERS))[1:])
        ]
        return [arrays[0], *reversed(sent)]

    slots_in = jnp.concatenate(send(list(slots_out.reshape(groups, capacity))))
    outgoing = rotate(held, where, comp_ops, comp_sectors, place, capacity, groups, CHUNKS)
    received = []
    for k in range(len(CHUNKS)):
        received.append(send(outgoing[k * groups : (k + 1) * groups]))
    pieces = []
    for k in range(len(CHUNKS)):
        partial = combine(received[k], slots_in, terms)
        parts = exchange(partial, TERM)
        pieces.append(jnp.sum(parts.astype(jnp.float32), axis=0).astype(jnp.bfloat16))
    comp_rotated = jnp.concatenate(pieces, axis=0).reshape(1, 1, width, width)

    tiles = norm_ops.shape[0]
    ids = jnp.arange(tiles, dtype=jnp.int32)
    (normal,) = rotate(held, where, norm_ops, norm_sectors, ids, tiles, 1, (width,))
    return normal, comp_rotated


def solution(mesh):
    cut = Mesh(mesh.devices.reshape(SIZES), AXES)
    return jax.shard_map(
        step,
        mesh=cut,
        in_specs=(
            P(AXES, None),
            P(AXES, None, None),
            P(AXES, None),
            P(AXES, None, None),
            P(AXES, None),
            P(AXES, None),
            P(AXES),
        ),
        out_specs=(P(AXES, None, None), P(("yhi", "core"), TERM, None, None)),
        check_vma=False,
    )
```
